256 devices in a mesh: seq: 32 (over y, z), mp: 8 (over x, core).
Axes of the slice: x: 4, y: 4, z: 8, core: 2. Of those that a mesh axis runs over, the one named last changes fastest.
Arguments:
- hidden: bfloat16 [4, 16384, 8192], P(None, 'seq', 'mp'), may hold values from -1000 to 1000
- norm_gain: bfloat16 [4, 8192], P(None, 'mp'), may hold values from 0.25 to 1.75
- proj_weight: bfloat16 [4, 8192, 1024], P(None, 'mp'), may hold values from -0.0625 to 0.0625
- start_block: bfloat16 [8, 512, 128], replicated, may hold values from -6 to 6
Outputs:
- latents: bfloat16 [16384, 8, 128], P('seq', 'mp')
The draws below stay inside these ranges and needn't reach their ends.
All inputs are finite; a program needn't handle non-finite values.
Results may differ from the reference program's by a relative error of at most 0.025.
Values may be sent and summed in bfloat16 or wider, within the bound.
A program may use at most 64 MiB of HBM per device.

```python
import jax
import jax.numpy as jnp
from jax import lax

D = 8192
HEADS = 4
HD = 128
LAYERS = 4
RANK = 128
ITERS = 2
PREFIX_TOKENS = 16384
STREAMS = 8
N_MP = 8


def draw_hidden(key, part):
    subkeys = jax.random.split(key, 4)
    position = jnp.arange(D, dtype=jnp.float32) / D
    jitter = jnp.exp(jax.random.uniform(subkeys[2], (D,), jnp.float32, -0.35, 0.35))
    common = jax.random.normal(subkeys[0], (PREFIX_TOKENS, D), jnp.float32)
    own_part = jax.random.normal(subkeys[1], (LAYERS, PREFIX_TOKENS, D), jnp.float32)
    columns = 10.0 ** position * jitter
    row_scale = 10.0 ** jax.random.uniform(subkeys[3], (LAYERS, PREFIX_TOKENS, 1), jnp.float32, 0.0, 1.0)
    base_value = 0.6 * common[None, :, :] + 0.8 * own_part
    drawn = jnp.clip(base_value * columns[None, None, :] * row_scale, -1000.0, 1000.0)
    return drawn.astype(jnp.bfloat16)


def level_of(key, dims, cuts, smallest, high):
    loudness = 1.0
    for dim, shards_of in cuts:
        heights = jax.random.uniform(jax.random.fold_in(jax.random.fold_in(key, 6), dim), (shards_of,), jnp.float32, smallest / len(cuts), high / len(cuts))
        loudness = loudness * jnp.repeat(jnp.exp(heights), dims[dim] // shards_of).reshape((-1,) + (1,) * (len(dims) - 1 - dim))
    return loudness


def normal_values(stream_key, dims, deviation, bound, shards=(), held_as=jnp.bfloat16):
    result = deviation * jax.random.normal(stream_key, dims, jnp.float32)
    if shards:
        result = result * level_of(stream_key, dims, shards, -0.22, 0.18)
    return jnp.clip(result, -bound, bound).astype(held_as)


def setup_inputs(seed: int = 0) -> dict:
    keys = jax.random.split(jax.random.key(seed), 5)
    hidden = draw_hidden(jax.random.fold_in(keys[4], 71), 0)
    norm_gain = jnp.clip(1.0 + 0.15 * jax.random.normal(keys[1], (LAYERS, D), jnp.float32), 0.25, 1.75).astype(jnp.bfloat16)
    proj_weight = normal_values(keys[2], (LAYERS, D, STREAMS * HD), D ** -0.5, 0.0625, ((1, 8),))
    start_block = normal_values(keys[3], (STREAMS, LAYERS * HD, RANK), 1.0, 6.0)
    return dict(hidden=hidden, norm_gain=norm_gain, proj_weight=proj_weight, start_block=start_block)


epsilon = 1e-05
highest_precision = lax.Precision.HIGHEST

def orthonormal_basis(image_block):
    inner_block = jnp.einsum('sar,saq->srq', image_block, image_block, precision=highest_precision)
    lower_factor = jnp.linalg.cholesky(inner_block)
    solved = jax.scipy.linalg.solve_triangular(lower_factor, jnp.swapaxes(image_block, 1, 2), lower=True)
    return jnp.swapaxes(solved, 1, 2)

def reference(hidden, norm_gain, proj_weight, start_block):
    width_here = D // N_MP
    layer_keys = []
    for layer in range(LAYERS):
        rows_full = hidden[layer].astype(jnp.float32)
        mean_square = lax.optimization_barrier(jnp.mean(rows_full * rows_full, axis=1, keepdims=True))
        normed = (rows_full * lax.rsqrt(mean_square + epsilon) * norm_gain[layer].astype(jnp.float32)[None, :]).astype(jnp.bfloat16)
        running = jnp.zeros((PREFIX_TOKENS, 2 * HEADS * HD), jnp.float32)
        for block_index in range(N_MP):
            first_col = block_index * width_here
            partial_sum = jnp.dot(normed[:, first_col:first_col + width_here].astype(jnp.float32), proj_weight[layer, first_col:first_col + width_here, :].astype(jnp.float32), preferred_element_type=jnp.float32)
            rounded = lax.optimization_barrier(partial_sum.astype(jnp.bfloat16))
            running = running + rounded.astype(jnp.float32)
        layer_keys.append(running.astype(jnp.bfloat16).reshape(PREFIX_TOKENS, 2 * HEADS, HD))
    stacked = jnp.stack(layer_keys, axis=2).reshape(PREFIX_TOKENS, 2 * HEADS, LAYERS * HD)
    widened = stacked.astype(jnp.float32)
    total_gram_matrix = jnp.einsum('tsa,tsb->sab', widened, widened, precision=highest_precision)
    block_of_basis = start_block.astype(jnp.float32)
    for repeat in range(ITERS):
        block_of_basis = orthonormal_basis(jnp.einsum('zcv,zvt->zct', total_gram_matrix, block_of_basis, precision=highest_precision))
    basis_half = block_of_basis.astype(jnp.bfloat16)
    return jnp.einsum('tsa,sar->tsr', widened, basis_half.astype(jnp.float32), precision=highest_precision).astype(jnp.bfloat16)
```

```python
import jax
import jax.numpy as jnp
from jax import lax
from jax.experimental import pallas as pl
from jax.experimental.pallas import tpu as pltpu
from jax.sharding import PartitionSpec as P

D = 8192
HD = 128
ITERS = 2
LAYERS = 4
NX, NY, NZ = 4, 4, 8
TOK = 512
HALF = TOK // 2
WIDTH = 1024
COLS = LAYERS * HD
LAG = 2
DEPTH = 4

epsilon = 1e-05
highest_precision = lax.Precision.HIGHEST
F32 = jnp.float32
BF16 = jnp.bfloat16


def wide(value):
    return value.astype(F32)


def exchange_kernel(
    hid, gain, weight, out_stacked, out_gram,
    gain_wide, hbuf, wbuf, parts, rcv, x2, xp, xm, rx2, fin,
    lane_sums, sq, sq_rcv, sq_pair, sq_x, row_factor,
    gram_wide, gram_send, ry, zsend, zwide, rz, gfin,
    h_sem, w_sem, pair_s, pair_r, x2_s, x2_r, fin_s, fin_r,
    sqp_s, sqp_r, sqx_s, sqx_r, y_s, y_r, z_s, z_r, gz_s, gz_r, gy_s, gy_r,
):
    seq = lax.axis_index("seq")
    mp = lax.axis_index("mp")
    y, z = seq // NZ, seq % NZ
    x, core = mp // 2, mp % 2

    def at_x(dx):
        return (seq, ((x + dx) % NX) * 2 + core)

    partner = (seq, x * 2 + (1 - core))

    def at_y(dy):
        return (((y + dy) % NY) * NZ + z, mp)

    def at_z(dz):
        return (y * NZ + (z + dz) % NZ, mp)

    def remote(src, dst, s_sem, r_sem, device):
        return pltpu.make_async_remote_copy(
            src_ref=src, dst_ref=dst, send_sem=s_sem, recv_sem=r_sem,
            device_id=device, device_id_type=pl.DeviceIdType.MESH,
        )

    def load_h(l):
        return pltpu.make_async_copy(hid.at[l], hbuf.at[l], h_sem.at[l])

    def load_w(i):
        k, l = i // LAYERS, i % LAYERS
        shift = jnp.where(k == 0, 2, jnp.where(k == 1, 1, jnp.where(k == 2, 3, 0)))
        target = (x + shift) % NX
        start = pl.multiple_of(target * (2 * HD), 2 * HD)
        return pltpu.make_async_copy(weight.at[l, :, pl.ds(start, 2 * HD)], wbuf.at[i], w_sem.at[i])

    for l in range(LAYERS):
        load_h(l).start()
        load_w(l).start()
    barrier = pltpu.get_barrier_semaphore()
    peers = [partner] + [at_x(d) for d in range(1, NX)] + [at_y(d) for d in range(1, NY)] + [at_z(d) for d in range(1, NZ)]
    for peer in peers:
        pl.semaphore_signal(barrier, inc=1, device_id=peer, device_id_type=pl.DeviceIdType.MESH)

    all_gains = wide(gain[...])
    for l in range(LAYERS):
        gain_wide[l] = jnp.broadcast_to(all_gains[l:l + 1, :], (8, WIDTH))

    def pair_copy(i):
        return remote(parts.at[i, 1 - core], rcv.at[i], pair_s.at[i], pair_r.at[i], partner)

    def x2_copy(side, l):
        rows = pl.ds(side * HALF, HALF)
        return remote(x2.at[l, rows], rx2.at[side, l], x2_s.at[side, l], x2_r.at[side, l], at_x(1 if side == 0 else NX - 1))

    def fin_copy(side, half, l):
        rows = pl.ds(half * HALF, HALF)
        source = xp if side == 0 else xm
        return remote(
            source.at[l, rows], fin.at[side, l, rows], fin_s.at[side, half, l], fin_r.at[side, half, l],
            at_x(1 if side == 0 else NX - 1),
        )

    def pair_sum(i, rows):
        return wide(parts[i, core, rows]) + wide(rcv[i, rows])

    ONE = pl.ds(0, HALF)
    TWO = pl.ds(HALF, HALF)

    def scale_rows(l):
        gains = gain_wide[l, 0:1, :]

        def block(b, carry):
            rows = pl.ds(pl.multiple_of(b * 64, 64), 64)
            h = wide(hbuf[l, rows, :])
            square = h * h
            total = square[:, 0:128]
            for c in range(1, WIDTH // 128):
                total = total + square[:, c * 128:(c + 1) * 128]
            lane_sums[l, rows, :] = total
            hbuf[l, rows, :] = (h * gains).astype(BF16)
            return carry

        lax.fori_loop(0, TOK // 64, block, 0)

    def chunk(i, carry):
        l = i % LAYERS

        @pl.when(i < LAYERS)
        def _():
            load_h(l).wait()
            scale_rows(l)

        load_w(i).wait()

        @pl.when(i + DEPTH < 4 * LAYERS)
        def _():
            load_w(i + DEPTH).start()

        for half in range(2):
            rows = pl.ds(half * HALF, HALF)
            product = jnp.dot(hbuf[l, rows, :], wbuf[i], preferred_element_type=F32)
            parts[i, 0, rows] = product[:, :HD].astype(BF16)
            parts[i, 1, rows] = product[:, HD:].astype(BF16)

        @pl.when(i == 0)
        def _():
            pl.semaphore_wait(barrier, len(peers))

        pair_copy(i).start()

        j = i - LAG
        m = j % LAYERS

        @pl.when((j >= 0) & (j < 3 * LAYERS))
        def _():
            pair_copy(j).wait_recv()

        @pl.when((j >= 0) & (j < LAYERS))
        def _():
            x2[m] = pair_sum(j, pl.ds(0, TOK)).astype(BF16)
            x2_copy(0, m).start()
            x2_copy(1, m).start()

        @pl.when((j >= LAYERS) & (j < 2 * LAYERS))
        def _():
            xp[m, TWO] = pair_sum(j, TWO).astype(BF16)
            fin_copy(0, 1, m).start()

        @pl.when((j >= 2 * LAYERS) & (j < 3 * LAYERS))
        def _():
            xm[m, ONE] = pair_sum(j, ONE).astype(BF16)
            fin_copy(1, 0, m).start()

        return carry

    lax.fori_loop(0, 4 * LAYERS, chunk, 0)

    row_id = lax.broadcasted_iota(jnp.int32, (8, HD), 0)

    def one_row(r):
        return jnp.where(row_id == r, 1.0, 0.0).astype(F32)

    squares = jnp.zeros((8, HALF), F32)
    for l in range(LAYERS):
        for half in range(2):
            squares = squares + lax.dot_general(
                one_row(half * LAYERS + l), lane_sums[l, half * HALF:(half + 1) * HALF, :],
                (((1,), (1,)), ((), ())), precision=highest_precision, preferred_element_type=F32,
            )
    sq[...] = squares
    sqp = remote(sq, sq_rcv, sqp_s, sqp_r, partner)
    sqp.start()

    def dependent(l, carry):
        x2_copy(0, l).wait_recv()
        xp[l, ONE] = (pair_sum(LAYERS + l, ONE) + wide(rx2[0, l])).astype(BF16)
        fin_copy(0, 0, l).start()
        x2_copy(1, l).wait_recv()
        xm[l, TWO] = (pair_sum(2 * LAYERS + l, TWO) + wide(rx2[1, l])).astype(BF16)
        fin_copy(1, 1, l).start()
        return carry

    sqp.wait_recv()
    sq_pair[...] = sq[...] + sq_rcv[...]
    sqx = [remote(sq_pair, sq_x.at[d - 1], sqx_s.at[d - 1], sqx_r.at[d - 1], at_x(d)) for d in range(1, NX)]
    for copy in sqx:
        copy.start()

    lax.fori_loop(0, LAYERS, dependent, 0)

    for copy in sqx:
        copy.wait_recv()
    total = sq_pair[...] + sq_x[0] + sq_x[1] + sq_x[2]
    factor = lax.rsqrt(total / D + epsilon)
    for l in range(LAYERS):
        for half in range(2):
            row_factor[l, half * HALF:(half + 1) * HALF, :] = lax.dot_general(
                factor, one_row(half * LAYERS + l),
                (((0,), (0,)), ((), ())), precision=highest_precision, preferred_element_type=F32,
            )

    for l in range(LAYERS):
        pair_copy(3 * LAYERS + l).wait_recv()
        for side in range(2):
            for half in range(2):
                fin_copy(side, half, l).wait_recv()
        everything = pl.ds(0, TOK)
        total = pair_sum(3 * LAYERS + l, everything) + wide(fin[0, l]) + wide(fin[1, l])
        out_stacked[:, l * HD:(l + 1) * HD] = (total * row_factor[l]).astype(BF16)

    for b in range(LAYERS):
        panel = lax.dot_general(
            out_stacked[...], out_stacked[:, b * HD:(b + 1) * HD], (((0,), (0,)), ((), ())), preferred_element_type=F32
        )
        gram_wide[b] = panel
        gram_send[b] = panel.astype(BF16)

    ys = [remote(gram_send.at[(y + d) % NY], ry.at[d - 1], y_s.at[d - 1], y_r.at[d - 1], at_y(d)) for d in range(1, NY)]
    for copy in ys:
        copy.start()
    for copy in ys:
        copy.wait_recv()
    summed = gram_wide[y] + wide(ry[0]) + wide(ry[1]) + wide(ry[2])
    zwide[...] = summed
    zsend[...] = summed.astype(BF16)
    ZR = COLS // NZ

    def z_rows(which):
        return pl.ds(pl.multiple_of(which * ZR, ZR), ZR)

    zs = [
        remote(zsend.at[z_rows((z + d) % NZ)], rz.at[d - 1], z_s.at[d - 1], z_r.at[d - 1], at_z(d))
        for d in range(1, NZ)
    ]
    for copy in zs:
        copy.start()
    for copy in zs:
        copy.wait_recv()
    summed = zwide[z_rows(z)]
    for d in range(1, NZ):
        summed = summed + wide(rz[d - 1])
    gfin[y, z_rows(z)] = summed.astype(BF16)

    gz_out = [
        remote(gfin.at[y, z_rows(z)], gfin.at[y, z_rows(z)], gz_s.at[d - 1], gz_r.at[d - 1], at_z(d))
        for d in range(1, NZ)
    ]
    gz_in = [
        remote(gfin.at[y, z_rows(z)], gfin.at[y, z_rows((z + NZ - d) % NZ)], gz_s.at[d - 1], gz_r.at[d - 1], at_z(d))
        for d in range(1, NZ)
    ]
    for copy in gz_out:
        copy.start()
    for copy in gz_in:
        copy.wait_recv()
    gy_out = [remote(gfin.at[y], gfin.at[y], gy_s.at[d - 1], gy_r.at[d - 1], at_y(d)) for d in range(1, NY)]
    gy_in = [remote(gfin.at[y], gfin.at[(y + NY - d) % NY], gy_s.at[d - 1], gy_r.at[d - 1], at_y(d)) for d in range(1, NY)]
    for copy in gy_out:
        copy.start()
    for copy in gy_in:
        copy.wait_recv()
    for b in range(LAYERS):
        out_gram[:, b * HD:(b + 1) * HD] = gfin[b]

    def drain(i, carry):
        pair_copy(i).wait_send()
        return carry

    lax.fori_loop(0, 4 * LAYERS, drain, 0)

    def drain_x(l, carry):
        for side in range(2):
            x2_copy(side, l).wait_send()
            for half in range(2):
                fin_copy(side, half, l).wait_send()
        return carry

    lax.fori_loop(0, LAYERS, drain_x, 0)
    for copy in [sqp] + sqx + ys + zs + gz_out + gy_out:
        copy.wait_send()


def exchange(hidden, norm_gain, proj_weight):
    dma = pltpu.SemaphoreType.DMA
    vmem = pltpu.VMEM
    return pl.pallas_call(
        exchange_kernel,
        out_shape=(jax.ShapeDtypeStruct((TOK, COLS), BF16), jax.ShapeDtypeStruct((COLS, COLS), BF16)),
        in_specs=[
            pl.BlockSpec(memory_space=pl.ANY),
            pl.BlockSpec(memory_space=pltpu.VMEM),
            pl.BlockSpec(memory_space=pl.ANY),
        ],
        out_specs=(pl.BlockSpec(memory_space=pltpu.VMEM), pl.BlockSpec(memory_space=pltpu.VMEM)),
        scratch_shapes=[
            vmem((LAYERS, 8, WIDTH), F32),
            vmem((LAYERS, TOK, WIDTH), BF16),
            vmem((16, WIDTH, 2 * HD), BF16),
            vmem((16, 2, TOK, HD), BF16),
            vmem((16, TOK, HD), BF16),
            vmem((LAYERS, TOK, HD), BF16),
            vmem((LAYERS, TOK, HD), BF16),
            vmem((LAYERS, TOK, HD), BF16),
            vmem((2, LAYERS, HALF, HD), BF16),
            vmem((2, LAYERS, TOK, HD), BF16),
            vmem((LAYERS, TOK, HD), F32),
            vmem((8, HALF), F32),
            vmem((8, HALF), F32),
            vmem((8, HALF), F32),
            vmem((NX - 1, 8, HALF), F32),
            vmem((LAYERS, TOK, HD), F32),
            vmem((LAYERS, COLS, HD), F32),
            vmem((LAYERS, COLS, HD), BF16),
            vmem((NY - 1, COLS, HD), BF16),
            vmem((COLS, HD), BF16),
            vmem((COLS, HD), F32),
            vmem((NZ - 1, COLS // NZ, HD), BF16),
            vmem((NY, COLS, HD), BF16),
            dma((LAYERS,)), dma((16,)), dma((16,)), dma((16,)),
            dma((2, LAYERS)), dma((2, LAYERS)), dma((2, 2, LAYERS)), dma((2, 2, LAYERS)),
            dma, dma, dma((NX - 1,)), dma((NX - 1,)),
            dma((NY - 1,)), dma((NY - 1,)), dma((NZ - 1,)), dma((NZ - 1,)),
            dma((NZ - 1,)), dma((NZ - 1,)), dma((NY - 1,)), dma((NY - 1,)),
        ],
        compiler_params=pltpu.CompilerParams(
            collective_id=0, has_side_effects=True, vmem_limit_bytes=56 * 1024 * 1024
        ),
    )(hidden, norm_gain, proj_weight)


def orthonormal_basis(image_block):
    inner_block = jnp.einsum("sar,saq->srq", image_block, image_block, precision=highest_precision)
    lower_factor = jnp.linalg.cholesky(inner_block)
    solved = jax.scipy.linalg.solve_triangular(
        lower_factor, jnp.swapaxes(image_block, 1, 2), lower=True
    )
    return jnp.swapaxes(solved, 1, 2)


def on_device(hidden, norm_gain, proj_weight, start_block):
    stacked, gram = exchange(hidden, norm_gain, proj_weight)
    block_of_basis = lax.dynamic_slice_in_dim(start_block, lax.axis_index("mp"), 1, 0).astype(F32)
    total_gram_matrix = gram.astype(F32)[None]
    for repeat in range(ITERS):
        block_of_basis = orthonormal_basis(
            jnp.einsum("zcv,zvt->zct", total_gram_matrix, block_of_basis, precision=highest_precision)
        )
    basis_half = block_of_basis.astype(BF16)
    return jnp.einsum("sta,sar->tsr", stacked[None], basis_half, preferred_element_type=F32).astype(BF16)


def solution(mesh):
    return jax.shard_map(
        on_device,
        mesh=mesh,
        in_specs=(P(None, "seq", "mp"), P(None, "mp"), P(None, "mp", None), P()),
        out_specs=P("seq", "mp", None),
        check_vma=False,
    )
```

```python
import jax
import jax.numpy as jnp
from jax import lax
from jax.experimental import pallas as pl
from jax.experimental.pallas import tpu as pltpu
from jax.sharding import PartitionSpec as P

D = 8192
HD = 128
ITERS = 2
LAYERS = 4
NX, NY, NZ = 4, 4, 8
TOK = 512
HALF = TOK // 2
WIDTH = 1024
COLS = LAYERS * HD
LAG = 2
DEPTH = 4

epsilon = 1e-05
highest_precision = lax.Precision.HIGHEST
F32 = jnp.float32
BF16 = jnp.bfloat16


def wide(value):
    return value.astype(F32)


def product(a, b, contract_a, contract_b, precision=None):
    return lax.dot_general(
        a, b, (((contract_a,), (contract_b,)), ((), ())), precision=precision, preferred_element_type=F32
    )


def inverse_cholesky(inner):
    n = inner.shape[0]
    lane = lax.broadcasted_iota(jnp.int32, (8, n), 1)
    sub = lax.broadcasted_iota(jnp.int32, (8, n), 0)
    blocks = [inner[8 * i:8 * i + 8] for i in range(n // 8)]
    for v in range(n // 8):
        first = 8 * v
        pivot_columns = (lane >= first) & (lane < first + 8)
        column = [jnp.broadcast_to(blocks[v][:, first + t:first + t + 1], (8, n)) for t in range(8)]
        s = [[column[t][i:i + 1, :] for t in range(i + 1)] for i in range(8)]
        row = [
            jnp.where(pivot_columns[0:1], jnp.where(lane[0:1] == first + t, 1.0, 0.0), blocks[v][t:t + 1, :])
            for t in range(8)
        ]
        inverse = [None] * 8
        m = [[None] * 8 for _ in range(8)]
        for t in range(8):
            inverse[t] = 1.0 / s[t][t]
            for i in range(t + 1, 8):
                m[i][t] = s[i][t] * inverse[t]
            for i in range(t + 1, 8):
                for u in range(t + 1, i + 1):
                    s[i][u] = s[i][u] - m[i][t] * s[u][t]
            for i in range(t + 1, 8):
                row[i] = row[i] - m[i][t] * row[t]
        scaled = [row[t] * inverse[t] for t in range(8)]
        done = blocks[v]
        for t in range(8):
            done = jnp.where(sub == t, jnp.where(lane[0:1] == first + t, s[t][t], row[t]), done)
        blocks[v] = done
        for k in range(v + 1, n // 8):
            old = [jnp.broadcast_to(blocks[k][:, first + t:first + t + 1], (8, n)) for t in range(8)]
            new = jnp.where(pivot_columns, 0.0, blocks[k])
            for t in range(8):
                for u in range(t):
                    old[t] = old[t] - m[t][u] * old[u]
                new = new - old[t] * scaled[t]
            blocks[k] = new
    rows = []
    for k in range(n // 8):
        diagonal = lane == sub + 8 * k
        pivots = jnp.sum(jnp.where(diagonal, blocks[k], 0.0), axis=1, keepdims=True)
        unit = jnp.where(lane < sub + 8 * k, blocks[k], jnp.where(diagonal, 1.0, 0.0))
        rows.append(unit * lax.rsqrt(pivots))
    return jnp.concatenate(rows, axis=0)


def exchange_kernel(
    hid, gain, weight, start, out,
    stacked, gram, start_here, basis, image,
    gain_wide, hbuf, wbuf, parts, rcv, x2, xp, xm, rx2, fin,
    lane_sums, sq, sq_rcv, sq_pair, sq_x, row_factor,
    gram_wide, gram_send, ry, zsend, zwide, rz, gfin,
    b_sem, h_sem, w_sem, pair_s, pair_r, x2_s, x2_r, fin_s, fin_r,
    sqp_s, sqp_r, sqx_s, sqx_r, y_s, y_r, z_s, z_r, gz_s, gz_r, gy_s, gy_r,
):
    seq = lax.axis_index("seq")
    mp = lax.axis_index("mp")
    y, z = seq // NZ, seq % NZ
    x, core = mp // 2, mp % 2

    def at_x(dx):
        return (seq, ((x + dx) % NX) * 2 + core)

    partner = (seq, x * 2 + (1 - core))

    def at_y(dy):
        return (((y + dy) % NY) * NZ + z, mp)

    def at_z(dz):
        return (y * NZ + (z + dz) % NZ, mp)

    def remote(src, dst, s_sem, r_sem, device):
        return pltpu.make_async_remote_copy(
            src_ref=src, dst_ref=dst, send_sem=s_sem, recv_sem=r_sem,
            device_id=device, device_id_type=pl.DeviceIdType.MESH,
        )

    def load_h(l):
        return pltpu.make_async_copy(hid.at[l], hbuf.at[l], h_sem.at[l])

    def load_w(i):
        k, l = i // LAYERS, i % LAYERS
        shift = jnp.where(k == 0, 2, jnp.where(k == 1, 1, jnp.where(k == 2, 3, 0)))
        target = (x + shift) % NX
        start = pl.multiple_of(target * (2 * HD), 2 * HD)
        return pltpu.make_async_copy(weight.at[l, :, pl.ds(start, 2 * HD)], wbuf.at[i], w_sem.at[i])

    for l in range(LAYERS):
        load_h(l).start()
        load_w(l).start()
    load_start = pltpu.make_async_copy(start.at[mp], start_here, b_sem)
    load_start.start()
    barrier = pltpu.get_barrier_semaphore()
    peers = [partner] + [at_x(d) for d in range(1, NX)] + [at_y(d) for d in range(1, NY)] + [at_z(d) for d in range(1, NZ)]
    for peer in peers:
        pl.semaphore_signal(barrier, inc=1, device_id=peer, device_id_type=pl.DeviceIdType.MESH)

    all_gains = wide(gain[...])
    for l in range(LAYERS):
        gain_wide[l] = jnp.broadcast_to(all_gains[l:l + 1, :], (8, WIDTH))

    def pair_copy(i):
        return remote(parts.at[i, 1 - core], rcv.at[i], pair_s.at[i], pair_r.at[i], partner)

    def x2_copy(side, l):
        rows = pl.ds(side * HALF, HALF)
        return remote(x2.at[l, rows], rx2.at[side, l], x2_s.at[side, l], x2_r.at[side, l], at_x(1 if side == 0 else NX - 1))

    def fin_copy(side, half, l):
        rows = pl.ds(half * HALF, HALF)
        source = xp if side == 0 else xm
        return remote(
            source.at[l, rows], fin.at[side, l, rows], fin_s.at[side, half, l], fin_r.at[side, half, l],
            at_x(1 if side == 0 else NX - 1),
        )

    def pair_sum(i, rows):
        return wide(parts[i, core, rows]) + wide(rcv[i, rows])

    ONE = pl.ds(0, HALF)
    TWO = pl.ds(HALF, HALF)

    def scale_rows(l):
        gains = gain_wide[l, 0:1, :]

        def block(b, carry):
            rows = pl.ds(pl.multiple_of(b * 64, 64), 64)
            h = wide(hbuf[l, rows, :])
            square = h * h
            total = square[:, 0:128]
            for c in range(1, WIDTH // 128):
                total = total + square[:, c * 128:(c + 1) * 128]
            lane_sums[l, rows, :] = total
            hbuf[l, rows, :] = (h * gains).astype(BF16)
            return carry

        lax.fori_loop(0, TOK // 64, block, 0)

    def chunk(i, carry):
        l = i % LAYERS

        @pl.when(i < LAYERS)
        def _():
            load_h(l).wait()
            scale_rows(l)

        load_w(i).wait()

        @pl.when(i + DEPTH < 4 * LAYERS)
        def _():
            load_w(i + DEPTH).start()

        for half in range(2):
            rows = pl.ds(half * HALF, HALF)
            product = jnp.dot(hbuf[l, rows, :], wbuf[i], preferred_element_type=F32)
            parts[i, 0, rows] = product[:, :HD].astype(BF16)
            parts[i, 1, rows] = product[:, HD:].astype(BF16)

        @pl.when(i == 0)
        def _():
            pl.semaphore_wait(barrier, len(peers))

        pair_copy(i).start()

        j = i - LAG
        m = j % LAYERS

        @pl.when((j >= 0) & (j < 3 * LAYERS))
        def _():
            pair_copy(j).wait_recv()

        @pl.when((j >= 0) & (j < LAYERS))
        def _():
            x2[m] = pair_sum(j, pl.ds(0, TOK)).astype(BF16)
            x2_copy(0, m).start()
            x2_copy(1, m).start()

        @pl.when((j >= LAYERS) & (j < 2 * LAYERS))
        def _():
            xp[m, TWO] = pair_sum(j, TWO).astype(BF16)
            fin_copy(0, 1, m).start()

        @pl.when((j >= 2 * LAYERS) & (j < 3 * LAYERS))
        def _():
            xm[m, ONE] = pair_sum(j, ONE).astype(BF16)
            fin_copy(1, 0, m).start()

        return carry

    lax.fori_loop(0, 4 * LAYERS, chunk, 0)

    row_id = lax.broadcasted_iota(jnp.int32, (8, HD), 0)

    def one_row(r):
        return jnp.where(row_id == r, 1.0, 0.0).astype(F32)

    squares = jnp.zeros((8, HALF), F32)
    for l in range(LAYERS):
        for half in range(2):
            squares = squares + lax.dot_general(
                one_row(half * LAYERS + l), lane_sums[l, half * HALF:(half + 1) * HALF, :],
                (((1,), (1,)), ((), ())), precision=highest_precision, preferred_element_type=F32,
            )
    sq[...] = squares
    sqp = remote(sq, sq_rcv, sqp_s, sqp_r, partner)
    sqp.start()

    def dependent(l, carry):
        x2_copy(0, l).wait_recv()
        xp[l, ONE] = (pair_sum(LAYERS + l, ONE) + wide(rx2[0, l])).astype(BF16)
        fin_copy(0, 0, l).start()
        x2_copy(1, l).wait_recv()
        xm[l, TWO] = (pair_sum(2 * LAYERS + l, TWO) + wide(rx2[1, l])).astype(BF16)
        fin_copy(1, 1, l).start()
        return carry

    sqp.wait_recv()
    sq_pair[...] = sq[...] + sq_rcv[...]
    sqx = [remote(sq_pair, sq_x.at[d - 1], sqx_s.at[d - 1], sqx_r.at[d - 1], at_x(d)) for d in range(1, NX)]
    for copy in sqx:
        copy.start()

    lax.fori_loop(0, LAYERS, dependent, 0)

    for copy in sqx:
        copy.wait_recv()
    total = sq_pair[...] + sq_x[0] + sq_x[1] + sq_x[2]
    factor = lax.rsqrt(total / D + epsilon)
    for l in range(LAYERS):
        for half in range(2):
            row_factor[l, half * HALF:(half + 1) * HALF, :] = lax.dot_general(
                factor, one_row(half * LAYERS + l),
                (((0,), (0,)), ((), ())), precision=highest_precision, preferred_element_type=F32,
            )

    for l in range(LAYERS):
        pair_copy(3 * LAYERS + l).wait_recv()
        for side in range(2):
            for half in range(2):
                fin_copy(side, half, l).wait_recv()
        everything = pl.ds(0, TOK)
        total = pair_sum(3 * LAYERS + l, everything) + wide(fin[0, l]) + wide(fin[1, l])
        stacked[:, l * HD:(l + 1) * HD] = (total * row_factor[l]).astype(BF16)

    for b in range(LAYERS):
        panel = lax.dot_general(
            stacked[...], stacked[:, b * HD:(b + 1) * HD], (((0,), (0,)), ((), ())), preferred_element_type=F32
        )
        gram_wide[b] = panel
        gram_send[b] = panel.astype(BF16)

    ys = [remote(gram_send.at[(y + d) % NY], ry.at[d - 1], y_s.at[d - 1], y_r.at[d - 1], at_y(d)) for d in range(1, NY)]
    for copy in ys:
        copy.start()
    for copy in ys:
        copy.wait_recv()
    summed = gram_wide[y] + wide(ry[0]) + wide(ry[1]) + wide(ry[2])
    zwide[...] = summed
    zsend[...] = summed.astype(BF16)
    ZR = COLS // NZ

    def z_rows(which):
        return pl.ds(pl.multiple_of(which * ZR, ZR), ZR)

    zs = [
        remote(zsend.at[z_rows((z + d) % NZ)], rz.at[d - 1], z_s.at[d - 1], z_r.at[d - 1], at_z(d))
        for d in range(1, NZ)
    ]
    for copy in zs:
        copy.start()
    for copy in zs:
        copy.wait_recv()
    summed = zwide[z_rows(z)]
    for d in range(1, NZ):
        summed = summed + wide(rz[d - 1])
    gfin[y, z_rows(z)] = summed.astype(BF16)

    gz_out = [
        remote(gfin.at[y, z_rows(z)], gfin.at[y, z_rows(z)], gz_s.at[d - 1], gz_r.at[d - 1], at_z(d))
        for d in range(1, NZ)
    ]
    gz_in = [
        remote(gfin.at[y, z_rows(z)], gfin.at[y, z_rows((z + NZ - d) % NZ)], gz_s.at[d - 1], gz_r.at[d - 1], at_z(d))
        for d in range(1, NZ)
    ]
    for copy in gz_out:
        copy.start()
    for copy in gz_in:
        copy.wait_recv()
    gy_out = [remote(gfin.at[y], gfin.at[y], gy_s.at[d - 1], gy_r.at[d - 1], at_y(d)) for d in range(1, NY)]
    gy_in = [remote(gfin.at[y], gfin.at[(y + NY - d) % NY], gy_s.at[d - 1], gy_r.at[d - 1], at_y(d)) for d in range(1, NY)]
    for copy in gy_out:
        copy.start()
    for copy in gy_in:
        copy.wait_recv()
    for b in range(LAYERS):
        gram[:, b * HD:(b + 1) * HD] = gfin[b]

    load_start.wait()
    basis[...] = wide(start_here[...])

    def power_step(repeat, carry):
        held = basis[...]
        high = held.astype(BF16)
        rest = held - wide(high)
        middle = rest.astype(BF16)
        low = (rest - wide(middle)).astype(BF16)
        whole = gram[...]
        image[...] = product(whole, high, 1, 0) + product(whole, middle, 1, 0) + product(whole, low, 1, 0)
        inner = product(image[...], image[...], 0, 0, highest_precision)
        basis[...] = product(image[...], inverse_cholesky(inner), 1, 1, highest_precision)
        return carry

    lax.fori_loop(0, ITERS, power_step, 0)
    out[...] = product(stacked[...], basis[...].astype(BF16), 1, 0).astype(BF16)

    def drain(i, carry):
        pair_copy(i).wait_send()
        return carry

    lax.fori_loop(0, 4 * LAYERS, drain, 0)

    def drain_x(l, carry):
        for side in range(2):
            x2_copy(side, l).wait_send()
            for half in range(2):
                fin_copy(side, half, l).wait_send()
        return carry

    lax.fori_loop(0, LAYERS, drain_x, 0)
    for copy in [sqp] + sqx + ys + zs + gz_out + gy_out:
        copy.wait_send()


def on_device(hidden, norm_gain, proj_weight, start_block):
    dma = pltpu.SemaphoreType.DMA
    vmem = pltpu.VMEM
    latents = pl.pallas_call(
        exchange_kernel,
        out_shape=jax.ShapeDtypeStruct((TOK, HD), BF16),
        in_specs=[
            pl.BlockSpec(memory_space=pl.ANY),
            pl.BlockSpec(memory_space=pltpu.VMEM),
            pl.BlockSpec(memory_space=pl.ANY),
            pl.BlockSpec(memory_space=pl.ANY),
        ],
        out_specs=pl.BlockSpec(memory_space=pltpu.VMEM),
        scratch_shapes=[
            vmem((TOK, COLS), BF16),
            vmem((COLS, COLS), BF16),
            vmem((COLS, HD), BF16),
            vmem((COLS, HD), F32),
            vmem((COLS, HD), F32),
            vmem((LAYERS, 8, WIDTH), F32),
            vmem((LAYERS, TOK, WIDTH), BF16),
            vmem((16, WIDTH, 2 * HD), BF16),
            vmem((16, 2, TOK, HD), BF16),
            vmem((16, TOK, HD), BF16),
            vmem((LAYERS, TOK, HD), BF16),
            vmem((LAYERS, TOK, HD), BF16),
            vmem((LAYERS, TOK, HD), BF16),
            vmem((2, LAYERS, HALF, HD), BF16),
            vmem((2, LAYERS, TOK, HD), BF16),
            vmem((LAYERS, TOK, HD), F32),
            vmem((8, HALF), F32),
            vmem((8, HALF), F32),
            vmem((8, HALF), F32),
            vmem((NX - 1, 8, HALF), F32),
            vmem((LAYERS, TOK, HD), F32),
            vmem((LAYERS, COLS, HD), F32),
            vmem((LAYERS, COLS, HD), BF16),
            vmem((NY - 1, COLS, HD), BF16),
            vmem((COLS, HD), BF16),
            vmem((COLS, HD), F32),
            vmem((NZ - 1, COLS // NZ, HD), BF16),
            vmem((NY, COLS, HD), BF16),
            dma, dma((LAYERS,)), dma((16,)), dma((16,)), dma((16,)),
            dma((2, LAYERS)), dma((2, LAYERS)), dma((2, 2, LAYERS)), dma((2, 2, LAYERS)),
            dma, dma, dma((NX - 1,)), dma((NX - 1,)),
            dma((NY - 1,)), dma((NY - 1,)), dma((NZ - 1,)), dma((NZ - 1,)),
            dma((NZ - 1,)), dma((NZ - 1,)), dma((NY - 1,)), dma((NY - 1,)),
        ],
        compiler_params=pltpu.CompilerParams(
            collective_id=0, has_side_effects=True, vmem_limit_bytes=56 * 1024 * 1024
        ),
    )(hidden, norm_gain, proj_weight, start_block)
    return latents.reshape(TOK, 1, HD)


def solution(mesh):
    return jax.shard_map(
        on_device,
        mesh=mesh,
        in_specs=(P(None, "seq", "mp"), P(None, "mp"), P(None, "mp", None), P()),
        out_specs=P("seq", "mp", None),
        check_vma=False,
    )
```
